32 devices in a mesh: wide: 16 (over z, y, x), col: 2 (over core).
Axes of the slice: x: 2, y: 2, z: 4, core: 2. Of those that a mesh axis runs over, the one named last changes fastest.
Arguments:
- phi_values: bfloat16 [16, 2, 8, 384, 512], P('wide', 'col'), may hold values from -1.5 to 1.5
- density: bfloat16 [32, 4, 128, 128], P('wide', 'col'), may hold values from -3.5 to 3.5
- lnv_matrix: bfloat16 [32, 4, 128, 128], P('wide', 'col'), may hold values from -0.1875 to 0.1875
- core_density: float32 [32, 32, 128], P('wide', 'col'), may hold values from 0.5 to 2
- pair_owner: int32 [16, 2, 72, 1], P('wide', 'col'), may hold values from 0 to 15; in each aligned block of 72 rows (0 to 71, 72 to 143, ..., all dimensions but the last counted through in order) at most 6 rows name the same one
- pair_source: int32 [16, 2, 72], P('wide', 'col'), may hold values from 0 to 3
- term_left: int32 [32, 4, 8], P('wide', 'col'), may hold values from 0 to 3
- term_right: int32 [32, 4, 8], P('wide', 'col'), may hold values from 0 to 11
Outputs:
- potential: float32 [32, 32, 128], P('wide', 'col')
- hamiltonian: float32 [32, 4, 128, 128], P('wide', 'col')
- gradient: float32 [32, 4, 128, 128], P('wide', 'col')
The draws below stay inside these ranges and needn't reach their ends.
Inputs may be any that keep to these rules, and one draw needn't show every extreme that they name: `pair_owner`: within the 72 pairs of one device no owner is named more than 6 times, and some device names some owner exactly 6 times.
All inputs are finite; a program needn't handle non-finite values.
Results may differ from the reference program's by a relative error of at most 0.0051.
Values may be sent and summed in bfloat16 or wider, within the bound.
No kernel may reach another device: no remote copies, remote signals or barrier semaphores. Data moves between devices by JAX's collectives and lax.ppermute only.
A program may use at most 64 MiB of HBM per device.

```python
import math
import jax
import jax.numpy as jnp
import numpy as np
from jax import lax

OB = 128
TILES_DEV = 8
TX = 2
TY = 16
TZT = 16
BR_DEV = 2
NZ_DEV = 2
NTERM = 8
NLOC = 4
NBLK = 32
NNZ = 4
SLABS = 16
STRIPS = 2
NPAIR = 72
CAP = 6
TZ = 128
PT = 512
NX = 32
NY = 32
N_WIDE = 16


def plant(values, stream_key, low, high):
    extent = values.shape
    place = [jax.random.randint(jax.random.fold_in(stream_key, axis), (), 0, extent[axis]) for axis in range(len(extent))]
    values = values.at[tuple(place)].set(low)
    longest = extent.index(max(extent))
    place[longest] = (place[longest] + 1) % extent[longest]
    return values.at[tuple(place)].set(high)


def block_levels(key, extent, cuts, low, largest):
    gain = 1.0
    for position, shards_of in cuts:
        steps = jax.random.uniform(jax.random.fold_in(jax.random.fold_in(key, 6), position), (shards_of,), jnp.float32, low / len(cuts), largest / len(cuts))
        gain = gain * jnp.repeat(jnp.exp(steps), extent[position] // shards_of).reshape((-1,) + (1,) * (len(extent) - 1 - position))
    return gain


def deal_out(key, own, number, rows, count, top, most, skew):
    sequence = jax.random.permutation(key, count)
    heavy_load, common = load_shares(count, rows * top, most, skew, True), load_shares(count, rows * top, most, skew, False)
    places = jnp.arange(count)

    def named(sizes, turn):
        used = int((sizes > 0).sum())
        fixed = max(1, used // 4)
        shifted = fixed + (places - fixed + turn * (used - fixed)) % max(1, count - fixed)
        return jnp.zeros((count,), jnp.int32).at[sequence[jnp.where(places < fixed, places, shifted)]].set(jnp.asarray(sizes, jnp.int32))

    sizes = jnp.where(number % 4 == 0, named(heavy_load, number // 4), named(common, number - number // 4 - 1))
    mixed = jax.random.permutation(jax.random.fold_in(own, 3), count)
    source_of, receiver = mixed[0:count // 2 * 2:2], mixed[1:count // 2 * 2:2]
    slack = jnp.minimum(sizes[source_of] - 1, most - sizes[receiver]) // 2
    slack = jnp.where((source_of == sequence[0]) | (receiver == sequence[0]) | (sizes[receiver] == 0), 0, jnp.maximum(slack, 0))
    shifted = jax.random.randint(jax.random.fold_in(own, 4), (count // 2,), 0, 1 << 20) % (slack + 1)
    sizes = sizes.at[source_of].add(-shifted).at[receiver].add(shifted)
    items = jnp.searchsorted(jnp.cumsum(sizes), jnp.arange(rows * top), side="right").astype(jnp.int32)
    listing = items.reshape(top, rows).T
    listing = listing[jax.random.permutation(jax.random.fold_in(own, 1), rows)]
    turn = jax.random.randint(jax.random.fold_in(own, 2), (rows, 1), 0, top)
    return jnp.take_along_axis(listing, (jnp.arange(top)[None, :] + turn) % top, axis=1)


def load_shares(amount, total, limit, lean, full):
    portions = [(1 << 20) // math.isqrt(standing ** lean) + 1 for standing in range(1, amount + 1)]
    largest = limit if full else min(limit, max(-(-total // amount), total * portions[0] // sum(portions)))
    least = 1 if total - largest >= amount - 1 else 0
    counts, rest = [largest] + [least] * (amount - 1), total - largest - least * (amount - 1)
    while rest > 0:
        candidates = [i for i in range(1, amount) if counts[i] < largest] or [i for i in range(1, amount) if counts[i] < limit]
        pool, remaining = sum([portions[i] for i in candidates]), rest
        for i in candidates:
            more = min(limit - counts[i], max(1, remaining * portions[i] // pool), rest)
            counts[i] = counts[i] + more
            rest = rest - more
    return np.array(counts)


def centred(key, shape, spread, most, cuts=(), kind=jnp.bfloat16):
    array = spread * jax.random.normal(key, shape, jnp.float32)
    if cuts:
        array = array * block_levels(key, shape, cuts, -0.22, 0.18)
    return jnp.clip(array, -most, most).astype(kind)


def setup_inputs(seed: int = 0) -> dict:
    splits = jax.random.split(jax.random.key(seed), 9)
    phi_values = centred(splits[0], (SLABS, STRIPS, TILES_DEV, 3 * OB, PT), (0.5 / (TX * TY * TZT) ** 0.25), 1.5, ((0, 16), (1, 2)))
    density = centred(splits[1], (NBLK, NNZ, OB, OB), (4.0 * (TX * TY * TZT) ** 0.5 / (3 * OB)), 3.5, ((0, 16), (1, 2)))
    lnv_matrix = centred(splits[2], (NBLK, NNZ, OB, OB), (NTERM * OB) ** -0.5, 0.1875, ((0, 16), (1, 2)))
    core_density = jnp.clip(jnp.exp(math.log(2.0) - 1.3862944 * jax.random.uniform(splits[3], (NX, NY, TZ), jnp.float32) ** block_levels(splits[3], (NX, NY, TZ), ((0, 16), (1, 2)), -0.2, 0.2)), 0.5, 2.0)
    pair_owner_keys = jax.random.split(jax.random.fold_in(splits[4], 1), SLABS * STRIPS * NPAIR // NPAIR)
    pair_owner_turns = jax.random.permutation(jax.random.fold_in(splits[4], 3), SLABS * STRIPS * NPAIR // NPAIR)
    pair_owner = jax.vmap(lambda own, number: deal_out(jax.random.fold_in(splits[4], 2), own, number, NPAIR, N_WIDE, 1, CAP, 2))(pair_owner_keys, pair_owner_turns).reshape((SLABS, STRIPS, NPAIR, 1))
    pair_source = plant(jax.random.randint(splits[5], (SLABS, STRIPS, NPAIR), 0, NLOC), jax.random.fold_in(splits[5], 1), 0, NLOC - 1).astype(jnp.int32)
    term_left = plant(jax.random.randint(splits[6], (NBLK, NNZ, NTERM), 0, NNZ), jax.random.fold_in(splits[6], 1), 0, NNZ - 1).astype(jnp.int32)
    term_right = plant(jax.random.randint(splits[7], (NBLK, NNZ, NTERM), 0, 3 * NLOC), jax.random.fold_in(splits[7], 1), 0, (3 * NLOC) - 1).astype(jnp.int32)
    return {"phi_values": phi_values, "density": density, "lnv_matrix": lnv_matrix, "core_density": core_density, "pair_owner": pair_owner, "pair_source": pair_source, "term_left": term_left, "term_right": term_right}


SPACING = 0.1
ENHANCE_LIMIT = 0.804
GRADIENT_COEFF = 0.2195

def exchange_energy(smooth, grad_sq):
    fermi_sq = (3.0 * jnp.pi ** 2) ** (2.0 / 3.0)
    reduced = grad_sq / (4.0 * fermi_sq * smooth ** (8.0 / 3.0))
    enhance = 1.0 + ENHANCE_LIMIT - ENHANCE_LIMIT / (1.0 + GRADIENT_COEFF * reduced / ENHANCE_LIMIT)
    return -0.75 * (3.0 / jnp.pi) ** (1.0 / 3.0) * smooth ** (4.0 / 3.0) * enhance

def total_energy(charge, core_density):
    smooth = jnp.sqrt(charge * charge + core_density * core_density)
    grad_sq = jnp.zeros_like(charge)
    for axis_id in range(3):
        slope = (jnp.roll(charge, -1, axis_id) - jnp.roll(charge, 1, axis_id)) / (2.0 * SPACING)
        grad_sq = grad_sq + slope * slope
    return jnp.sum(exchange_energy(smooth, grad_sq))

def block_place(owners, sources, strip):
    row_index = owners * BR_DEV + sources // NZ_DEV
    slot_index = strip * NZ_DEV + sources % NZ_DEV
    return (row_index, slot_index)

def tiles_to_field(values):
    return values.reshape(TILES_DEV, TX, TY, TZT).transpose(1, 2, 0, 3).reshape(TX, TY, TZ)

def field_to_tiles(field):
    return field.reshape(TX, TY, TILES_DEV, TZT).transpose(2, 0, 1, 3).reshape(TILES_DEV, PT)

def sparse_product(left_blocks, right_blocks, term_left, term_right):
    slot_strip = jnp.arange(NNZ, dtype=jnp.int32) // NZ_DEV

    def one_row(inputs):
        row_id, left_row, lefts, rights = inputs
        window_row = (row_id // BR_DEV * BR_DEV - BR_DEV + rights // NZ_DEV) % NBLK
        window_slot = slot_strip[:, None] * NZ_DEV + rights % NZ_DEV
        chosen_right = right_blocks[window_row, window_slot].astype(jnp.float32)
        chosen_left = left_row[lefts].astype(jnp.float32)
        return jnp.einsum('jtab,jtbc->jac', chosen_left, chosen_right, precision=lax.Precision.HIGHEST)
    return lax.map(one_row, (jnp.arange(NBLK, dtype=jnp.int32), left_blocks, term_left, term_right))

def reference(phi_values, density, lnv_matrix, core_density, pair_owner, pair_source, term_left, term_right):
    devices = SLABS * STRIPS
    phi_all = phi_values.reshape(devices, TILES_DEV, 3 * OB, PT)
    owners = pair_owner.reshape(devices, NPAIR)
    sources = pair_source.reshape(devices, NPAIR)
    strips = jnp.arange(devices, dtype=jnp.int32) % STRIPS

    def grid_density(inputs):
        orbital_values, owner_row, source_row, strip = inputs
        row_index, slot_index = block_place(owner_row, source_row, strip)
        blocks = density[row_index, slot_index]
        tile_matrix = blocks.reshape(TILES_DEV, 3, 3, OB, OB).transpose(0, 1, 3, 2, 4).reshape(TILES_DEV, 3 * OB, 3 * OB)
        values = orbital_values.astype(jnp.float32)
        applied = jnp.einsum('tij,tjp->tip', tile_matrix.astype(jnp.float32), values, precision=lax.Precision.HIGHEST)
        return tiles_to_field(lax.optimization_barrier(jnp.sum(values * applied, axis=1)))
    fields = lax.map(grid_density, (phi_all, owners, sources, strips))
    charge = fields.reshape(SLABS, STRIPS, TX, TY, TZ).transpose(0, 2, 1, 3, 4).reshape(NX, NY, TZ)
    potential = jax.grad(total_energy)(charge, core_density)
    local_pot = potential.reshape(SLABS, TX, STRIPS, TY, TZ).transpose(0, 2, 1, 3, 4).reshape(devices, TX, TY, TZ)

    def add_parts(hamiltonian, inputs):
        orbital_values, owner_row, source_row, strip, field = inputs
        voltage = field_to_tiles(field)
        values = orbital_values.astype(jnp.float32)
        weighted = (values * voltage[:, None, :]).astype(jnp.bfloat16)
        tile_ham = jnp.einsum('tip,tjp->tij', weighted.astype(jnp.float32), values, precision=lax.Precision.HIGHEST)
        pieces = tile_ham.reshape(TILES_DEV, 3, OB, 3, OB).transpose(0, 1, 3, 2, 4).reshape(NPAIR, OB, OB)
        pieces = lax.optimization_barrier(pieces.astype(jnp.bfloat16)).astype(jnp.float32)
        row_index, slot_index = block_place(owner_row, source_row, strip)
        return (hamiltonian.at[row_index, slot_index].add(pieces), None)
    hamiltonian, _ = lax.scan(add_parts, jnp.zeros((NBLK, NNZ, OB, OB), jnp.float32), (phi_all, owners, sources, strips, local_pot))
    first_term = sparse_product(lnv_matrix, hamiltonian.astype(jnp.bfloat16), term_left, term_right)
    second = sparse_product(lnv_matrix, first_term.astype(jnp.bfloat16), term_left, term_right)
    gradient = 3.0 * first_term - 2.0 * second
    return (potential, hamiltonian, gradient)
```

```python
import functools

import jax
import jax.numpy as jnp
from jax import lax
from jax.experimental import pallas as pl
from jax.experimental.pallas import tpu as pltpu
from jax.sharding import PartitionSpec as P

SPACING = 0.1
ENHANCE_LIMIT = 0.804
GRADIENT_COEFF = 0.2195
PLANE = 4
VMEM = pl.BlockSpec(memory_space=pltpu.VMEM)
SMEM = pl.BlockSpec(memory_space=pltpu.SMEM)
PARAMS = pltpu.CompilerParams(vmem_limit_bytes=32 * 1024 * 1024)


def swap(values, axis, mask):
    count = lax.axis_size(axis)
    return lax.ppermute(values, axis, [(i, i ^ mask) for i in range(count)])


def shift(values, axis, step):
    count = lax.axis_size(axis)
    return lax.ppermute(values, axis, [(i, (i + step) % count) for i in range(count)])


def padded_2(cells, axis, dim, width):
    count = lax.axis_size(axis)
    head = lax.slice_in_dim(cells, 0, width, axis=dim)
    tail = lax.slice_in_dim(cells, cells.shape[dim] - width, cells.shape[dim], axis=dim)
    if count == 2:
        other = swap(jnp.concatenate([head, tail], axis=dim), axis, 1)
        after = lax.slice_in_dim(other, 0, width, axis=dim)
        before = lax.slice_in_dim(other, width, 2 * width, axis=dim)
    else:
        before, after = shift(tail, axis, 1), shift(head, axis, -1)
    return jnp.concatenate([before, cells, after], axis=dim)


def exchange_energy(smooth, grad_sq):
    fermi_sq = (3.0 * jnp.pi**2) ** (2.0 / 3.0)
    reduced = grad_sq / (4.0 * fermi_sq * smooth ** (8.0 / 3.0))
    enhance = 1.0 + ENHANCE_LIMIT - ENHANCE_LIMIT / (1.0 + GRADIENT_COEFF * reduced / ENHANCE_LIMIT)
    return -0.75 * (3.0 / jnp.pi) ** (1.0 / 3.0) * smooth ** (4.0 / 3.0) * enhance


def cell_terms(charge, core_values, grad_first, grad_second):
    grad_third = (jnp.roll(charge, -1, 2) - jnp.roll(charge, 1, 2)) / (2.0 * SPACING)
    smooth = jnp.sqrt(charge * charge + core_values * core_values)
    grad_sq = grad_first * grad_first + grad_second * grad_second + grad_third * grad_third
    energy, pullback = jax.vjp(exchange_energy, smooth, grad_sq)
    slope_smooth, slope_grad = pullback(jnp.ones_like(energy))
    local_part = slope_smooth * charge / smooth
    return (
        local_part,
        2.0 * slope_grad * grad_first,
        2.0 * slope_grad * grad_second,
        2.0 * slope_grad * grad_third,
    )


def potential_of(charge, core_density):
    stacked = jnp.stack([charge, core_density])
    stacked = padded_2(padded_2(stacked, "wide", 1, 2), "col", 2, 2)
    padded = stacked[0]
    inner_charge = padded[1:-1, 1:-1]
    grad_first = (padded[2:, 1:-1] - padded[:-2, 1:-1]) / (2.0 * SPACING)
    grad_second = (padded[1:-1, 2:] - padded[1:-1, :-2]) / (2.0 * SPACING)
    local_ext, rim_first, rim_second, flux_ext = cell_terms(
        inner_charge, stacked[1][1:-1, 1:-1], grad_first, grad_second
    )
    flux_third = flux_ext[1:-1, 1:-1]
    divergence = (
        rim_first[:-2, 1:-1] - rim_first[2:, 1:-1] + rim_second[1:-1, :-2] - rim_second[1:-1, 2:]
    )
    divergence = divergence + jnp.roll(flux_third, 1, 2) - jnp.roll(flux_third, -1, 2)
    return local_ext[1:-1, 1:-1] + divergence / (2.0 * SPACING)


def gather_all(blocks):
    depth = lax.axis_size("wide") // PLANE
    ring = jnp.concatenate([blocks] + [swap(blocks, "wide", PLANE * s) for s in range(1, depth)])
    half = ring.shape[0] // 2
    low, high = ring[:half], ring[half:]
    low_x, high_y = swap(low, "wide", 1), swap(high, "wide", 2)
    low_y, high_x = swap(low, "wide", 2), swap(high, "wide", 1)
    low_xy, high_xy = swap(low_x, "wide", 2), swap(high_y, "wide", 1)
    return (ring, low_x, high_x, low_y, high_y, low_xy, high_xy)


def charge_kernel(slots, orbitals, *refs):
    pieces, (out, held) = refs[:-2], refs[-2:]
    at = 0
    for piece in pieces:
        held[at : at + piece.shape[0]] = piece[...]
        at += piece.shape[0]
    tiles = orbitals.shape[0]

    def tile(t, carry):
        values = orbitals[t]
        total = None
        width = held.shape[1]
        for a in range(3):
            row = jnp.concatenate([held[slots[9 * t + 3 * a + b]] for b in range(3)], axis=1)
            applied = jnp.dot(row, values, preferred_element_type=jnp.float32)
            mine = values[a * width : (a + 1) * width].astype(jnp.float32)
            part = jnp.sum(applied * mine, axis=0, keepdims=True)
            total = part if total is None else total + part
        out[pl.ds(t, 1), :] = total
        return carry

    lax.fori_loop(0, tiles, tile, 0)


def tile_charge_of(slots, orbitals, pieces):
    count = sum(p.shape[0] for p in pieces)
    return pl.pallas_call(
        charge_kernel,
        out_shape=jax.ShapeDtypeStruct((orbitals.shape[0], orbitals.shape[2]), jnp.float32),
        in_specs=[SMEM] + [VMEM] * (1 + len(pieces)),
        out_specs=VMEM,
        scratch_shapes=[pltpu.VMEM((count,) + pieces[0].shape[1:], jnp.bfloat16)],
        compiler_params=PARAMS,
    )(slots, orbitals, *pieces)


def ham_kernel(slots, orbitals, voltage, *refs):
    outs, total = refs[:-1], refs[-1]
    total[...] = jnp.zeros_like(total)
    width = total.shape[1]

    def tile(t, carry):
        values = orbitals[t]
        weighted = (values.astype(jnp.float32) * voltage[pl.ds(t, 1), :]).astype(jnp.bfloat16)
        product = lax.dot_general(
            weighted, values, (((1,), (1,)), ((), ())), preferred_element_type=jnp.float32
        )
        product = product.astype(jnp.bfloat16).astype(jnp.float32)
        for a in range(3):
            for b in range(3):
                slot = slots[9 * t + 3 * a + b]
                piece = product[a * width : (a + 1) * width, b * width : (b + 1) * width]
                total[slot] = total[slot] + piece
        return carry

    lax.fori_loop(0, orbitals.shape[0], tile, 0)
    at = 0
    for out in outs:
        out[...] = total[at : at + out.shape[0]].astype(out.dtype)
        at += out.shape[0]


def ham_parts(slots, orbitals, voltage, blocks, width):
    half = blocks // (2 * PLANE)
    kinds = [(2 * half, jnp.float32)]
    kinds += [(half, jnp.bfloat16), (half, jnp.float32), (half, jnp.float32)]
    kinds += [(half, jnp.bfloat16)] * 3
    return pl.pallas_call(
        ham_kernel,
        out_shape=[jax.ShapeDtypeStruct((k, width, width), d) for k, d in kinds],
        in_specs=[SMEM, VMEM, VMEM],
        out_specs=[VMEM] * len(kinds),
        scratch_shapes=[pltpu.VMEM((blocks, width, width), jnp.float32)],
        compiler_params=PARAMS,
    )(slots, orbitals, voltage)


def reduce_all(parts):
    own, low_x, high_x, low_y, high_y, low_xy, high_xy = parts
    wide = lambda v: v.astype(jnp.float32)
    depth = lax.axis_size("wide") // PLANE
    half = low_x.shape[0]
    from_x, from_y = swap(low_xy, "wide", 1), swap(high_xy, "wide", 2)
    low_x, high_y = swap(low_x, "wide", 1), swap(high_y, "wide", 2)
    low_y = swap((low_y + wide(from_x)).astype(jnp.bfloat16), "wide", 2)
    high_x = swap((high_x + wide(from_y)).astype(jnp.bfloat16), "wide", 1)
    low = own[:half] + wide(low_x) + wide(low_y)
    high = own[half:] + wide(high_x) + wide(high_y)
    planes = jnp.concatenate([low, high])
    planes = planes.reshape((depth, planes.shape[0] // depth) + planes.shape[1:])
    total = planes[0]
    for s in range(1, depth):
        total = total + wide(swap(planes[s].astype(jnp.bfloat16), "wide", PLANE * s))
    return total


def product_kernel(is_first, lefts, rights, left_blocks, before, own, after, *refs):
    window = refs[-1]
    count = own.shape[0]
    for k, piece in enumerate((before, own, after)):
        window[k * count : (k + 1) * count] = piece[...]
    terms = lefts.shape[0] // count
    for j in range(count):
        at = [j * terms + t for t in range(terms)]
        left = jnp.concatenate([left_blocks[lefts[i]] for i in at], axis=1)
        right = jnp.concatenate([window[rights[i]] for i in at], axis=0)
        summed = jnp.dot(left, right, preferred_element_type=jnp.float32)
        if is_first:
            refs[0][j] = summed
            refs[1][j] = summed.astype(jnp.bfloat16)
        else:
            refs[1][j] = 3.0 * refs[0][j] - 2.0 * summed


def product(lefts, rights, left_blocks, half, first=None):
    before, after = shift(half, "wide", 1), shift(half, "wide", -1)
    more = [] if first is None else [first]
    exact = jax.ShapeDtypeStruct(half.shape, jnp.float32)
    out = [exact, jax.ShapeDtypeStruct(half.shape, jnp.bfloat16)] if first is None else exact
    return pl.pallas_call(
        functools.partial(product_kernel, first is None),
        out_shape=out,
        in_specs=[SMEM, SMEM] + [VMEM] * (4 + len(more)),
        out_specs=[VMEM, VMEM] if first is None else VMEM,
        scratch_shapes=[pltpu.VMEM((3 * half.shape[0],) + half.shape[1:], jnp.bfloat16)],
        compiler_params=PARAMS,
    )(lefts, rights, left_blocks, before, half, after, *more)


def body(
    phi_values, density, lnv_matrix, core_density, pair_owner, pair_source, term_left, term_right
):
    orbital_values = phi_values[0, 0]
    tile_count = orbital_values.shape[0]
    width = density.shape[-1]
    block_rows, slot_count = (density.shape[0], density.shape[1])
    local_count = block_rows * slot_count
    slab_cells, strip_cells, depth_cells = core_density.shape
    depth_tile = depth_cells // tile_count
    owners = pair_owner[0, 0, :, 0]
    sources = pair_source[0, 0]
    slab_count = lax.axis_size("wide")
    strip_count = lax.axis_size("col")
    depth = slab_count // PLANE

    relative = owners ^ lax.axis_index("wide")
    slots = ((relative % PLANE) * depth + relative // PLANE) * local_count + sources
    pieces = gather_all(density.reshape(local_count, width, width))
    tile_charge = tile_charge_of(slots, orbital_values, pieces)
    charge = (
        tile_charge.reshape(tile_count, slab_cells, strip_cells, depth_tile)
        .transpose(1, 2, 0, 3)
        .reshape(slab_cells, strip_cells, depth_cells)
    )
    potential = potential_of(charge, core_density)
    voltage = (
        potential.reshape(slab_cells, strip_cells, tile_count, depth_tile)
        .transpose(2, 0, 1, 3)
        .reshape(tile_count, -1)
    )
    parts = ham_parts(slots, orbital_values, voltage, slab_count * local_count, width)
    hamiltonian = reduce_all(parts)

    local_lnv = lnv_matrix.reshape(local_count, width, width)
    left_blocks = jnp.concatenate(
        [local_lnv] + [swap(local_lnv, "col", s) for s in range(1, strip_count)]
    )
    strip = (term_left // slot_count) ^ lax.axis_index("col")
    row = jnp.arange(block_rows, dtype=jnp.int32)[:, None, None]
    lefts = (strip * local_count + row * slot_count + term_left % slot_count).reshape(-1)
    rights = term_right.reshape(-1)
    first_term, first_half = product(lefts, rights, left_blocks, hamiltonian.astype(jnp.bfloat16))
    gradient = product(lefts, rights, left_blocks, first_half, first_term)
    shape = (block_rows, slot_count, width, width)
    return (potential, hamiltonian.reshape(shape), gradient.reshape(shape))


def solution(mesh):
    in_specs = (
        P("wide", "col", None, None, None),
        P("wide", "col", None, None),
        P("wide", "col", None, None),
        P("wide", "col", None),
        P("wide", "col", None, None),
        P("wide", "col", None),
        P("wide", "col", None),
        P("wide", "col", None),
    )
    out_specs = (P("wide", "col", None), P("wide", "col", None, None), P("wide", "col", None, None))
    return jax.shard_map(body, mesh=mesh, in_specs=in_specs, out_specs=out_specs, check_vma=False)
```

```python
import functools

import jax
import jax.numpy as jnp
from jax import lax
from jax.experimental import pallas as pl
from jax.experimental.pallas import tpu as pltpu
from jax.sharding import PartitionSpec as P


SPACING = 0.1
ENHANCE_LIMIT = 0.804
GRADIENT_COEFF = 0.2195
PLANE = 4
STAGE_LIMIT = 48 * 1024 * 1024
VMEM = pl.BlockSpec(memory_space=pltpu.VMEM)
SMEM = pl.BlockSpec(memory_space=pltpu.SMEM)
PARAMS = pltpu.CompilerParams(vmem_limit_bytes=32 * 1024 * 1024)


def swap(values, axis, mask):
    count = lax.axis_size(axis)
    return lax.ppermute(values, axis, [(i, i ^ mask) for i in range(count)])


def joined(pieces):
    return pieces[0] if len(pieces) == 1 else jnp.concatenate(pieces)


def single(values):
    return values.astype(jnp.float32)


def shift(values, axis, step):
    count = lax.axis_size(axis)
    return lax.ppermute(values, axis, [(i, (i + step) % count) for i in range(count)])


def padded_2(cells, axis, dim, width):
    count = lax.axis_size(axis)
    head = lax.slice_in_dim(cells, 0, width, axis=dim)
    tail = lax.slice_in_dim(cells, cells.shape[dim] - width, cells.shape[dim], axis=dim)
    if count == 2:
        other = swap(jnp.concatenate([head, tail], axis=dim), axis, 1)
        after = lax.slice_in_dim(other, 0, width, axis=dim)
        before = lax.slice_in_dim(other, width, 2 * width, axis=dim)
    else:
        before, after = shift(tail, axis, 1), shift(head, axis, -1)
    return jnp.concatenate([before, cells, after], axis=dim)


def exchange_energy(smooth, grad_sq):
    fermi_sq = (3.0 * jnp.pi**2) ** (2.0 / 3.0)
    reduced = grad_sq / (4.0 * fermi_sq * smooth ** (8.0 / 3.0))
    enhance = 1.0 + ENHANCE_LIMIT - ENHANCE_LIMIT / (1.0 + GRADIENT_COEFF * reduced / ENHANCE_LIMIT)
    return -0.75 * (3.0 / jnp.pi) ** (1.0 / 3.0) * smooth ** (4.0 / 3.0) * enhance


def cell_terms(charge, core_values, grad_first, grad_second):
    grad_third = (jnp.roll(charge, -1, 2) - jnp.roll(charge, 1, 2)) / (2.0 * SPACING)
    smooth = jnp.sqrt(charge * charge + core_values * core_values)
    grad_sq = grad_first * grad_first + grad_second * grad_second + grad_third * grad_third
    energy, pullback = jax.vjp(exchange_energy, smooth, grad_sq)
    slope_smooth, slope_grad = pullback(jnp.ones_like(energy))
    local_part = slope_smooth * charge / smooth
    return (
        local_part,
        2.0 * slope_grad * grad_first,
        2.0 * slope_grad * grad_second,
        2.0 * slope_grad * grad_third,
    )


def potential_of(charge, core_density):
    stacked = jnp.stack([charge, core_density])
    stacked = padded_2(padded_2(stacked, "wide", 1, 2), "col", 2, 2)
    padded = stacked[0]
    inner_charge = padded[1:-1, 1:-1]
    grad_first = (padded[2:, 1:-1] - padded[:-2, 1:-1]) / (2.0 * SPACING)
    grad_second = (padded[1:-1, 2:] - padded[1:-1, :-2]) / (2.0 * SPACING)
    local_ext, rim_first, rim_second, flux_ext = cell_terms(
        inner_charge, stacked[1][1:-1, 1:-1], grad_first, grad_second
    )
    flux_third = flux_ext[1:-1, 1:-1]
    divergence = (
        rim_first[:-2, 1:-1] - rim_first[2:, 1:-1] + rim_second[1:-1, :-2] - rim_second[1:-1, 2:]
    )
    divergence = divergence + jnp.roll(flux_third, 1, 2) - jnp.roll(flux_third, -1, 2)
    return local_ext[1:-1, 1:-1] + divergence / (2.0 * SPACING)


def gather_all(blocks):
    depth = lax.axis_size("wide") // PLANE
    planes = [blocks]
    planes += [swap(blocks, "wide", PLANE * s) for s in range(1, depth)]
    step = depth // 4
    quarters = [joined(planes[step * q : step * (q + 1)]) for q in range(4)]
    from_x, from_y, from_xy = [], [], []
    for g in range(2):
        low, high = quarters[2 * g], quarters[2 * g + 1]
        low_x, high_y = swap(low, "wide", 1), swap(high, "wide", 2)
        low_y, high_x = swap(low, "wide", 2), swap(high, "wide", 1)
        low_xy, high_xy = swap(low_x, "wide", 2), swap(high_y, "wide", 1)
        from_x += [low_x, high_x]
        from_y += [low_y, high_y]
        from_xy += [low_xy, high_xy]
    return quarters + from_x + from_y + from_xy


def stage_kernel(orbitals, held, ready):
    copy = pltpu.make_async_copy(orbitals, held, ready)
    copy.start()
    copy.wait()


def staged(values):
    return pl.pallas_call(
        stage_kernel,
        out_shape=jax.ShapeDtypeStruct(values.shape, values.dtype),
        in_specs=[pl.BlockSpec(memory_space=pltpu.HBM)],
        out_specs=VMEM,
        scratch_shapes=[pltpu.SemaphoreType.DMA],
        compiler_params=pltpu.CompilerParams(vmem_limit_bytes=STAGE_LIMIT),
    )(values)


def charge_kernel(slots, orbitals, *refs):
    pieces, (out, held) = refs[:-2], refs[-2:]
    at = 0
    for piece in pieces:
        held[at : at + piece.shape[0]] = piece[...]
        at += piece.shape[0]
    tiles = orbitals.shape[0]

    def tile(t, carry):
        values = orbitals[t]
        total = None
        width = held.shape[1]
        for a in range(3):
            row = jnp.concatenate([held[slots[9 * t + 3 * a + b]] for b in range(3)], axis=1)
            applied = jnp.dot(row, values, preferred_element_type=jnp.float32)
            mine = values[a * width : (a + 1) * width].astype(jnp.float32)
            part = jnp.sum(applied * mine, axis=0, keepdims=True)
            total = part if total is None else total + part
        out[pl.ds(t, 1), :] = total
        return carry

    lax.fori_loop(0, tiles, tile, 0, unroll=8)


def tile_charge_of(slots, orbitals, pieces):
    count = sum(p.shape[0] for p in pieces)
    return pl.pallas_call(
        charge_kernel,
        out_shape=jax.ShapeDtypeStruct((orbitals.shape[0], orbitals.shape[2]), jnp.float32),
        in_specs=[SMEM] + [VMEM] * (1 + len(pieces)),
        out_specs=VMEM,
        scratch_shapes=[pltpu.VMEM((count,) + pieces[0].shape[1:], jnp.bfloat16)],
        compiler_params=PARAMS,
    )(slots, orbitals, *pieces)


def ham_kernel(slots, orbitals, voltage, *refs):
    outs, total = refs[:-1], refs[-1]
    total[...] = jnp.zeros_like(total)
    width = total.shape[1]

    def tile(t, carry):
        values = orbitals[t]
        weighted = (values.astype(jnp.float32) * voltage[pl.ds(t, 1), :]).astype(jnp.bfloat16)
        product = lax.dot_general(
            weighted, values, (((1,), (1,)), ((), ())), preferred_element_type=jnp.float32
        )
        product = product.astype(jnp.bfloat16).astype(jnp.float32)
        for a in range(3):
            for b in range(3):
                slot = slots[9 * t + 3 * a + b]
                piece = product[a * width : (a + 1) * width, b * width : (b + 1) * width]
                total[slot] = total[slot] + piece
        return carry

    lax.fori_loop(0, orbitals.shape[0], tile, 0, unroll=8)
    at = 0
    for out in outs:
        out[...] = total[at : at + out.shape[0]].astype(out.dtype)
        at += out.shape[0]


def ham_parts(slots, orbitals, voltage, blocks, width):
    count = blocks // (4 * PLANE)
    near, far = jnp.float32, jnp.bfloat16
    kinds = [near] * 4 + [far, near] * 2 + [near, far] * 2 + [far] * 4
    return pl.pallas_call(
        ham_kernel,
        out_shape=[jax.ShapeDtypeStruct((count, width, width), kind) for kind in kinds],
        in_specs=[SMEM, VMEM, VMEM],
        out_specs=[VMEM] * len(kinds),
        scratch_shapes=[pltpu.VMEM((blocks, width, width), jnp.float32)],
        compiler_params=PARAMS,
    )(slots, orbitals, voltage)


def reduce_all(parts):
    own, to_x, to_y, to_xy = parts[:4], parts[4:8], parts[8:12], parts[12:]
    depth = lax.axis_size("wide") // PLANE
    step = depth // 4
    total = [None] * depth
    for g in (1, 0):
        a, b = 2 * g, 2 * g + 1
        low_c, high_c = swap(to_xy[a], "wide", 1), swap(to_xy[b], "wide", 2)
        low_x, high_y = swap(to_x[a], "wide", 1), swap(to_y[b], "wide", 2)
        low_y = swap((to_y[a] + single(low_c)).astype(jnp.bfloat16), "wide", 2)
        high_x = swap((to_x[b] + single(high_c)).astype(jnp.bfloat16), "wide", 1)
        for q, sums in (
            (a, own[a] + single(low_x) + single(low_y)),
            (b, own[b] + single(high_x) + single(high_y)),
        ):
            planes = sums.reshape((step, sums.shape[0] // step) + sums.shape[1:])
            for k in range(step):
                s = q * step + k
                plane = planes[k]
                if s > 0:
                    sent = swap(plane.astype(jnp.bfloat16), "wide", PLANE * s)
                    plane = single(sent)
                total[s] = plane
    return total


def product_kernel(is_first, lefts, rights, left_blocks, before, own, after, *refs):
    window = refs[-1]
    count = own.shape[0]
    for k, piece in enumerate((before, own, after)):
        window[k * count : (k + 1) * count] = piece[...]
    terms = lefts.shape[0] // count
    for j in range(count):
        at = [j * terms + t for t in range(terms)]
        left = jnp.concatenate([left_blocks[lefts[i]] for i in at], axis=1)
        right = jnp.concatenate([window[rights[i]] for i in at], axis=0)
        summed = jnp.dot(left, right, preferred_element_type=jnp.float32)
        if is_first:
            refs[0][j] = summed
            refs[1][j] = summed.astype(jnp.bfloat16)
        else:
            refs[1][j] = 3.0 * refs[0][j] - 2.0 * summed


def product(lefts, rights, left_blocks, half, first=None):
    before, after = shift(half, "wide", 1), shift(half, "wide", -1)
    more = [] if first is None else [first]
    exact = jax.ShapeDtypeStruct(half.shape, jnp.float32)
    out = [exact, jax.ShapeDtypeStruct(half.shape, jnp.bfloat16)] if first is None else exact
    return pl.pallas_call(
        functools.partial(product_kernel, first is None),
        out_shape=out,
        in_specs=[SMEM, SMEM] + [VMEM] * (4 + len(more)),
        out_specs=[VMEM, VMEM] if first is None else VMEM,
        scratch_shapes=[pltpu.VMEM((3 * half.shape[0],) + half.shape[1:], jnp.bfloat16)],
        compiler_params=PARAMS,
    )(lefts, rights, left_blocks, before, half, after, *more)


def body(
    phi_values, density, lnv_matrix, core_density, pair_owner, pair_source, term_left, term_right
):
    orbital_values = phi_values[0, 0]
    tile_count = orbital_values.shape[0]
    width = density.shape[-1]
    block_rows, slot_count = (density.shape[0], density.shape[1])
    local_count = block_rows * slot_count
    slab_cells, strip_cells, depth_cells = core_density.shape
    depth_tile = depth_cells // tile_count
    owners = pair_owner[0, 0, :, 0]
    sources = pair_source[0, 0]
    slab_count = lax.axis_size("wide")
    strip_count = lax.axis_size("col")
    depth = slab_count // PLANE

    relative = owners ^ lax.axis_index("wide")
    beside = relative % PLANE
    turned = beside // 2 + beside % 2 * 2
    beside = jnp.where(lax.axis_index("col") % 2 == 1, turned, beside)
    slots = ((relative % PLANE) * depth + relative // PLANE) * local_count + sources
    ham_slots = slots
    pieces = gather_all(density.reshape(local_count, width, width))
    tile_charge = tile_charge_of(slots, staged(orbital_values), pieces)
    charge = (
        tile_charge.reshape(tile_count, slab_cells, strip_cells, depth_tile)
        .transpose(1, 2, 0, 3)
        .reshape(slab_cells, strip_cells, depth_cells)
    )
    potential = potential_of(charge, core_density)
    voltage = (
        potential.reshape(slab_cells, strip_cells, tile_count, depth_tile)
        .transpose(2, 0, 1, 3)
        .reshape(tile_count, -1)
    )
    parts = ham_parts(ham_slots, orbital_values, voltage, slab_count * local_count, width)
    terms = reduce_all(parts)
    half = sum(terms[1:], terms[0]).astype(jnp.bfloat16)

    local_lnv = lnv_matrix.reshape(local_count, width, width)
    left_blocks = jnp.concatenate(
        [local_lnv] + [swap(local_lnv, "col", s) for s in range(1, strip_count)]
    )
    strip = (term_left // slot_count) ^ lax.axis_index("col")
    row = jnp.arange(block_rows, dtype=jnp.int32)[:, None, None]
    lefts = (strip * local_count + row * slot_count + term_left % slot_count).reshape(-1)
    rights = term_right.reshape(-1)
    first_term, first_half = product(lefts, rights, left_blocks, half)
    terms, first_half = lax.optimization_barrier((terms, first_half))
    hamiltonian = sum(terms[1:], terms[0])
    gradient = product(lefts, rights, left_blocks, first_half, first_term)
    shape = (block_rows, slot_count, width, width)
    return (potential, hamiltonian.reshape(shape), gradient.reshape(shape))


def solution(mesh):
    in_specs = (
        P("wide", "col", None, None, None),
        P("wide", "col", None, None),
        P("wide", "col", None, None),
        P("wide", "col", None),
        P("wide", "col", None, None),
        P("wide", "col", None),
        P("wide", "col", None),
        P("wide", "col", None),
    )
    out_specs = (P("wide", "col", None), P("wide", "col", None, None), P("wide", "col", None, None))

    return jax.shard_map(body, mesh=mesh, in_specs=in_specs, out_specs=out_specs, check_vma=False)
```
